32 devices in a mesh: row: 2 (over x), col: 4 (over z), fit: 4 (over y, core).
Axes of the slice: x: 2, y: 2, z: 4, core: 2. Of those that a mesh axis runs over, the one named last changes fastest.
Arguments:
- orbital_ints: bfloat16 [16, 40, 2560], P(('row', 'col'), None, 'fit'), may hold values from -0.83984375 to 0.83984375
- occ_energy: float32 [16], P(('row', 'col')), may hold values from -1.2 to -0.3
- pair_row: int32 [1024], P(('row', 'col')), may hold values from 0 to 7
- pair_col: int32 [1024], P(('row', 'col')), may hold values from 0 to 3
- virt_energy: float32 [40, 1024], P(None, ('row', 'col')), may hold values from 0.5 to 3
- amplitudes: float32 [40, 40, 1024], P(None, None, ('row', 'col')), may hold values from -1.8 to 1.8
- intersections: bfloat16 [40, 40, 16, 1024], P(None, None, 'fit', ('row', 'col')), may hold values from -1 to 1
- coupling_fock: float32 [16, 1024], P('fit', ('row', 'col')), may hold values from -0.25 to 0.25
- partner_owner: int32 [4, 1024, 4], P('fit', ('row', 'col')), may hold values from 0 to 7, all different within a row; in each aligned block of 128 rows (0 to 127, 128 to 255, ..., all dimensions but the last counted through in order) at most 128 rows name the same one
- partner_slot: int32 [4, 1024, 4], P('fit', ('row', 'col')), may hold values from 0 to 127
Outputs:
- new_amplitudes: float32 [40, 40, 1024], P(None, None, ('row', 'col'))
- residual: float32 [40, 40, 1024], P(None, None, ('row', 'col'))
The draws below stay inside these ranges and needn't reach their ends.
Inputs may be any that keep to these rules, and one draw needn't show every extreme that they name: `partner_owner`: the 4 owners of one pair in one fit index differ; among the pairs of one group in one fit index (aligned blocks of 128 rows) no owner is named more than 128 times, a bound that some block reaches.
All inputs are finite; a program needn't handle non-finite values.
Results may differ from the reference program's by a relative error of at most 0.014.
Values may be sent and summed in bfloat16 or wider, within the bound.
A program may use at most 128 MiB of HBM per device.

```python
import math
import jax
import jax.numpy as jnp
import numpy as np
from jax import lax

NPNO = 40
NAUX = 2560
OCC_BLK = 2
PAIRS_DEV = 128
CPL_FIT = 4
ITERS = 2
OCC = 16
PAIRS = 1024
NCPL = 16
CAP = 128
N_ROW = 2
N_COL = 4
N_FIT = 4


def touch_ends(result, stream_key, low, largest):
    shape = result.shape
    spot = [jax.random.randint(jax.random.fold_in(stream_key, axis), (), 0, shape[axis]) for axis in range(len(shape))]
    result = result.at[tuple(spot)].set(low)
    longest = shape.index(max(shape))
    spot[longest] = (spot[longest] + 1) % shape[longest]
    return result.at[tuple(spot)].set(largest)


def level_of(own_key, shape, pieces, least, largest):
    factor_of, own = 1.0, jax.random.fold_in(own_key, 6)
    for position, parts in pieces:
        steps = jnp.exp(jax.random.uniform(jax.random.fold_in(own, position), (parts,), jnp.float32, least / len(pieces), largest / len(pieces)))
        factor_of = factor_of * jnp.repeat(steps, shape[position] // parts).reshape([-1 if axis == position else 1 for axis in range(len(shape))])
    return factor_of


def shared_out(own_key, own, number, rows, amount, top, most, slope):
    ranking = jax.random.permutation(own_key, amount)
    heavy_load, common = load_shares(amount, rows * top, most, slope, True), load_shares(amount, rows * top, most, slope, False)
    places = jnp.arange(amount)

    def named(tallies, rotation):
        used = int((tallies > 0).sum())
        fixed = max(1, used // 4)
        shifted = fixed + (places - fixed + rotation * (used - fixed)) % max(1, amount - fixed)
        return jnp.zeros((amount,), jnp.int32).at[ranking[jnp.where(places < fixed, places, shifted)]].set(jnp.asarray(tallies, jnp.int32))

    tallies = jnp.where(number % 4 == 0, named(heavy_load, number // 4), named(common, number - number // 4 - 1))
    mixed = jax.random.permutation(jax.random.fold_in(own, 3), amount)
    giver, receiver = mixed[0:amount // 2 * 2:2], mixed[1:amount // 2 * 2:2]
    margin = jnp.minimum(tallies[giver] - 1, most - tallies[receiver]) // 2
    margin = jnp.where((giver == ranking[0]) | (receiver == ranking[0]) | (tallies[receiver] == 0), 0, jnp.maximum(margin, 0))
    shifted = jax.random.randint(jax.random.fold_in(own, 4), (amount // 2,), 0, 1 << 20) % (margin + 1)
    tallies = tallies.at[giver].add(-shifted).at[receiver].add(shifted)
    items = jnp.searchsorted(jnp.cumsum(tallies), jnp.arange(rows * top), side="right").astype(jnp.int32)
    listing = items.reshape(top, rows).T
    listing = listing[jax.random.permutation(jax.random.fold_in(own, 1), rows)]
    rotation = jax.random.randint(jax.random.fold_in(own, 2), (rows, 1), 0, top)
    return jnp.take_along_axis(listing, (jnp.arange(top)[None, :] + rotation) % top, axis=1)


def load_shares(count, total, most, skew, full):
    portions = [(1 << 20) // math.isqrt(rank ** skew) + 1 for rank in range(1, count + 1)]
    largest = most if full else min(most, max(-(-total // count), total * portions[0] // sum(portions)))
    least = 1 if total - largest >= count - 1 else 0
    holding, surplus = [largest] + [least] * (count - 1), total - largest - least * (count - 1)
    while surplus > 0:
        free = [i for i in range(1, count) if holding[i] < largest] or [i for i in range(1, count) if holding[i] < most]
        pool, budget = sum([portions[i] for i in free]), surplus
        for i in free:
            addition = min(most - holding[i], max(1, budget * portions[i] // pool), surplus)
            holding[i] = holding[i] + addition
            surplus = surplus - addition
    return np.array(holding)


def centred(rng, extent, spread, limit, split=(), kind=jnp.bfloat16):
    values = jax.random.normal(rng, extent, jnp.float32) * spread
    if len(split) > 0:
        values = level_of(rng, extent, split, -0.22, 0.18) * values
    return jnp.clip(values, min=-limit, max=limit).astype(kind)


def setup_inputs(seed: int = 0) -> dict:
    streams_of = jax.random.split(jax.random.key(seed), 11)
    orbital_ints = centred(streams_of[0], (OCC, NPNO, NAUX), 0.14, 0.83984375, ((0, 8), (2, 4)))
    occ_energy = jnp.clip(-1.2 + 0.90000004 * jax.random.uniform(streams_of[1], (OCC,), jnp.float32) ** level_of(streams_of[1], (OCC,), ((0, 8),), -0.2, 0.2), -1.2, -0.3)
    pair_row = touch_ends(jax.random.randint(streams_of[2], (PAIRS,), 0, OCC // N_ROW), jax.random.fold_in(streams_of[2], 1), 0, (OCC // N_ROW) - 1).astype(jnp.int32)
    pair_col = touch_ends(jax.random.randint(streams_of[3], (PAIRS,), 0, OCC // N_COL), jax.random.fold_in(streams_of[3], 1), 0, (OCC // N_COL) - 1).astype(jnp.int32)
    virt_energy = jnp.clip(jnp.exp(math.log(3.0) - 1.7917595 * jax.random.uniform(streams_of[4], (NPNO, PAIRS), jnp.float32) ** level_of(streams_of[4], (NPNO, PAIRS), ((1, 8),), -0.2, 0.2)), 0.5, 3.0)
    amplitudes = centred(streams_of[5], (NPNO, NPNO, PAIRS), 0.3, 1.8, ((2, 8),), jnp.float32)
    intersections = centred(streams_of[6], (NPNO, NPNO, NCPL, PAIRS), NPNO ** -0.5, 1.0, ((2, 4), (3, 8)))
    coupling_fock = jnp.clip(jax.random.uniform(streams_of[7], (NCPL, PAIRS), jnp.float32, -0.25, 0.25) * level_of(streams_of[7], (NCPL, PAIRS), ((0, 4), (1, 8)), -0.4, 0.0), -0.25, 0.25)
    partner_owner_keys = jax.random.split(jax.random.fold_in(streams_of[8], 1), N_FIT * PAIRS // PAIRS_DEV)
    partner_owner_turns = jax.random.permutation(jax.random.fold_in(streams_of[8], 3), N_FIT * PAIRS // PAIRS_DEV)
    partner_owner = jax.vmap(lambda own, number: shared_out(jax.random.fold_in(streams_of[8], 2), own, number, PAIRS_DEV, N_ROW * N_COL, CPL_FIT, CAP, 2))(partner_owner_keys, partner_owner_turns).reshape((N_FIT, PAIRS, CPL_FIT))
    partner_slot = touch_ends(jax.random.randint(streams_of[9], (N_FIT, PAIRS, CPL_FIT), 0, PAIRS_DEV), jax.random.fold_in(streams_of[9], 1), 0, PAIRS_DEV - 1).astype(jnp.int32)
    return dict(orbital_ints=orbital_ints, occ_energy=occ_energy, pair_row=pair_row, pair_col=pair_col, virt_energy=virt_energy, amplitudes=amplitudes, intersections=intersections, coupling_fock=coupling_fock, partner_owner=partner_owner, partner_slot=partner_slot)


def reference(orbital_ints, occ_energy, pair_row, pair_col, virt_energy, amplitudes, intersections, coupling_fock, partner_owner, partner_slot):
    group_count = N_ROW * N_COL
    pair_index = jnp.arange(PAIRS, dtype=jnp.int32)
    group = pair_index // PAIRS_DEV
    row_of = group // N_COL
    col_of = group % N_COL
    first_orb = (row_of * (OCC // N_ROW) + pair_row).astype(jnp.int32)
    second_orb = (((pair_col // OCC_BLK) * N_COL + col_of) * OCC_BLK + pair_col % OCC_BLK).astype(jnp.int32)

    def kernel_group(indices):
        first_ints = orbital_ints[indices[0]].astype(jnp.float32)
        second_ints = orbital_ints[indices[1]].astype(jnp.float32)
        return jnp.einsum("pax,pbx->abp", first_ints, second_ints)

    stacked = lax.map(kernel_group, (first_orb.reshape(group_count, PAIRS_DEV), second_orb.reshape(group_count, PAIRS_DEV)))
    kernel = jnp.transpose(stacked, (1, 2, 0, 3)).reshape(NPNO, NPNO, PAIRS)
    denominator = virt_energy[:, None, :] + virt_energy[None, :, :] - (occ_energy[first_orb] + occ_energy[second_orb])[None, None, :]
    partner = jnp.transpose(partner_owner * PAIRS_DEV + partner_slot, (0, 2, 1)).reshape(NCPL, PAIRS)
    current = amplitudes
    residual = amplitudes
    for turn_index in range(ITERS):
        sent_tiles = current.astype(jnp.bfloat16)
        coupling = jnp.zeros((NPNO, NPNO, PAIRS), jnp.float32)
        for link in range(NCPL):
            tiles = sent_tiles[:, :, partner[link]].astype(jnp.float32)
            intersection = intersections[:, :, link, :].astype(jnp.float32)
            half_product = jnp.einsum("abp,bdp->adp", intersection, tiles).astype(jnp.bfloat16)
            coupled = jnp.einsum("adp,edp->aep", half_product.astype(jnp.float32), intersection)
            coupling = coupling + coupling_fock[link][None, None, :] * coupled
        residual = kernel + denominator * current - coupling
        current = current - residual / denominator
    return current, residual
```

```python
import functools

import jax
import jax.numpy as jnp
from jax import lax
from jax.experimental import pallas as pl
from jax.experimental.pallas import tpu as pltpu
from jax.sharding import PartitionSpec as P

ITERS = 2
LANES = 128
MESH = pl.DeviceIdType.MESH
ANY = pl.BlockSpec(memory_space=pl.ANY)
VMEM_LIMIT = 60 * 1024 * 1024


class Sender:
    def __init__(self, send_sems):
        self.send_sems, self.started = send_sems, []

    def send(self, source, target, recv_sem, device, when=None):
        copy = pltpu.make_async_remote_copy(
            src_ref=source,
            dst_ref=target,
            send_sem=self.send_sems.at[len(self.started)],
            recv_sem=recv_sem,
            device_id=device,
            device_id_type=MESH,
        )
        self.started.append((copy, when))
        guarded(when, copy.start)

    def finish(self):
        for copy, when in self.started:
            guarded(when, copy.wait_send)


def guarded(when, action):
    if when is None:
        action()
    else:
        pl.when(when)(action)


def both(first, second):
    return second if first is None else first if second is None else jnp.logical_and(first, second)


def greet(axes):
    barrier = pltpu.get_barrier_semaphore()
    total = 0
    for axis in axes:
        count = lax.axis_size(axis)
        here = lax.axis_index(axis)
        for step in range(1, count):
            pl.semaphore_signal(
                barrier, inc=1, device_id={axis: lax.rem(here + step, count)}, device_id_type=MESH
            )
            total += 1
    pl.semaphore_wait(barrier, total)


def gather_kernel(sizes, with_ints, *refs):
    if with_ints:
        own, ints, energy, tiles, row_ints, col_ints, row_en, col_en = refs[:8]
        send_sems, recv_sems, part_sems, int_sems, local_sems = refs[8:]
    else:
        own, tiles, send_sems, recv_sems, part_sems, local_sems = refs
    R, C = lax.axis_size("row"), lax.axis_size("col")
    r, c, f = lax.axis_index("row"), lax.axis_index("col"), lax.axis_index("fit")
    partner = {"fit": f + 1 - 2 * lax.rem(f, 2)}
    half = sum(sizes)
    mine = lax.rem(f, 2) * half
    theirs = half - mine
    me = r * C + c
    greet(("row", "col", "fit"))
    out = Sender(send_sems)
    offsets = (0, sizes[0])

    def place(piece, group, base=mine):
        return tiles.at[group, pl.ds(base + offsets[piece], sizes[piece])]

    def await_copy(piece, group, sem, base=mine, when=None):
        ref = place(piece, group, base)
        copy = pltpu.make_async_remote_copy(
            src_ref=ref, dst_ref=ref, send_sem=send_sems.at[0], recv_sem=sem,
            device_id=partner, device_id_type=MESH,
        )
        guarded(when, copy.wait_recv)

    def along(piece, group, step, when=None, source=None):
        inside = c + 1 < C if step > 0 else c > 0
        out.send(
            place(piece, group) if source is None else source, place(piece, group),
            recv_sems.at[piece, group], {"col": c + step}, both(when, inside),
        )

    def across(piece, group, when=None, source=None):
        for step in range(1, R):
            out.send(
                place(piece, group) if source is None else source, place(piece, group),
                recv_sems.at[piece, group], {"row": lax.rem(r + step, R)}, when,
            )

    def beside(piece, group, when=None):
        out.send(place(piece, group), place(piece, group), part_sems.at[piece, group], partner, when)

    def own_piece(piece):
        return own.at[pl.ds(mine + offsets[piece], sizes[piece])]

    across(1, me, source=own_piece(1))
    for step in (1, -1):
        along(0, me, step, source=own_piece(0))
    if with_ints:
        def int_wait(target, sem, when=None):
            copy = pltpu.make_async_remote_copy(
                src_ref=target, dst_ref=target, send_sem=send_sems.at[0], recv_sem=sem,
                device_id=partner, device_id_type=MESH,
            )
            guarded(when, copy.wait_recv)

        for step in (1, -1):
            inside = c + 1 < C if step > 0 else c > 0
            out.send(ints, row_ints.at[c], int_sems.at[0, c], {"col": c + step}, inside)
        for step in range(1, R):
            to = {"row": lax.rem(r + step, R)}
            out.send(ints, col_ints.at[r], int_sems.at[1, r], to)
            out.send(energy, col_en.at[r], int_sems.at[3, r], to)
        for step in range(1, C):
            to = {"col": lax.rem(c + step, C)}
            out.send(energy, row_en.at[c], int_sems.at[2, c], to)
    for step in (1, -1):
        along(1, me, step, source=own_piece(1))
    across(0, me, source=own_piece(0))
    local = [pltpu.make_async_copy(own, tiles.at[me], local_sems.at[0])]
    if with_ints:
        local += [
            pltpu.make_async_copy(ints, row_ints.at[c], local_sems.at[1]),
            pltpu.make_async_copy(ints, col_ints.at[r], local_sems.at[2]),
            pltpu.make_async_copy(energy, row_en.at[c], local_sems.at[3]),
            pltpu.make_async_copy(energy, col_en.at[r], local_sems.at[4]),
        ]
    for copy in local:
        copy.start()
    for other in range(1, R):
        group = lax.rem(r + other, R) * C + c
        await_copy(1, group, recv_sems.at[1, group])
        for step in (1, -1):
            along(1, group, step)
        beside(1, group)
    for distance in range(1, C):
        for step in (1, -1):
            source = c - step * distance
            there = jnp.logical_and(source >= 0, source < C)
            column = jnp.clip(source, 0, C - 1)
            group = r * C + column
            await_copy(0, group, recv_sems.at[0, group], when=there)
            if distance < C - 1:
                along(0, group, step, there)
            across(0, group, there)
            beside(0, group, there)
            for other in range(R):
                group = lax.rem(r + other, R) * C + column
                await_copy(1, group, recv_sems.at[1, group], when=there)
                if distance < C - 1:
                    along(1, group, step, there)
                beside(1, group, there)
            if with_ints:
                int_wait(row_ints.at[column], int_sems.at[0, column], there)
                if distance < C - 1:
                    inside = c + 1 < C if step > 0 else c > 0
                    out.send(
                        row_ints.at[column], row_ints.at[column], int_sems.at[0, column],
                        {"col": c + step}, both(there, inside),
                    )
    for other in range(1, R):
        for turn in range(C):
            group = lax.rem(r + other, R) * C + lax.rem(c + turn, C)
            await_copy(0, group, recv_sems.at[0, group])
            beside(0, group)
    if with_ints:
        for step in range(1, R):
            row = lax.rem(r + step, R)
            int_wait(col_ints.at[row], int_sems.at[1, row])
            int_wait(col_en.at[row], int_sems.at[3, row])
        for step in range(1, C):
            column = lax.rem(c + step, C)
            int_wait(row_en.at[column], int_sems.at[2, column])
    for step in range(1, R * C):
        group = lax.rem(me + step, R * C)
        for piece in range(2):
            await_copy(piece, group, part_sems.at[piece, group], base=theirs)
    for copy in local:
        copy.wait()
    out.finish()


def gather(packed, collective_id, ints=None, energy=None):
    R, C = lax.axis_size("row"), lax.axis_size("col")
    G = R * C
    with_ints = ints is not None
    half = packed.shape[0] // 2
    first = (half * 3 + 4) // 5
    shapes = [jax.ShapeDtypeStruct((G,) + packed.shape, packed.dtype)]
    operands = [packed]
    if with_ints:
        operands += [ints, energy]
        shapes += [
            jax.ShapeDtypeStruct((C,) + ints.shape, ints.dtype),
            jax.ShapeDtypeStruct((R,) + ints.shape, ints.dtype),
            jax.ShapeDtypeStruct((C,) + energy.shape, energy.dtype),
            jax.ShapeDtypeStruct((R,) + energy.shape, energy.dtype),
        ]
    scratch = [
        pltpu.SemaphoreType.DMA((16 * R * C + 32,)),
        pltpu.SemaphoreType.DMA((2, G)),
        pltpu.SemaphoreType.DMA((2, G)),
    ]
    if with_ints:
        scratch.append(pltpu.SemaphoreType.DMA((4, max(R, C))))
    scratch.append(pltpu.SemaphoreType.DMA((5,)))
    return pl.pallas_call(
        functools.partial(gather_kernel, (first, half - first), with_ints),
        out_shape=shapes,
        in_specs=[ANY] * len(operands),
        out_specs=[ANY] * len(shapes),
        scratch_shapes=scratch,
        name="gather_ints" if with_ints else "gather_tiles",
        compiler_params=pltpu.CompilerParams(
            collective_id=collective_id, has_side_effects=True, vmem_limit_bytes=VMEM_LIMIT
        ),
    )(*operands)


def sum_kernel(part, total, inbox, result, send_sems, recv_sems, gather_sems, local_sem):
    F = lax.axis_size("fit")
    f = lax.axis_index("fit")
    rows = part.shape[0] // F
    greet(("fit",))
    out = Sender(send_sems)
    for step in range(1, F):
        to = lax.rem(f + step, F)
        out.send(
            part.at[pl.ds(to * rows, rows)], inbox.at[step - 1], recv_sems.at[step - 1], {"fit": to}
        )
    value = part[pl.ds(f * rows, rows)].astype(jnp.float32)
    for step in range(1, F):
        pltpu.make_async_remote_copy(
            src_ref=inbox.at[step - 1], dst_ref=inbox.at[step - 1], send_sem=send_sems.at[0],
            recv_sem=recv_sems.at[step - 1], device_id={"fit": lax.rem(f + step, F)},
            device_id_type=MESH,
        ).wait_recv()
        value = value + inbox[step - 1].astype(jnp.float32)
    result[...] = value.astype(result.dtype)
    target = total.at[pl.ds(f * rows, rows)]
    for step in range(1, F):
        out.send(result, target, gather_sems.at[step - 1], {"fit": lax.rem(f + step, F)})
    local = pltpu.make_async_copy(result, target, local_sem)
    local.start()
    for step in range(1, F):
        source = lax.rem(f + F - step, F)
        ref = total.at[pl.ds(source * rows, rows)]
        pltpu.make_async_remote_copy(
            src_ref=ref, dst_ref=ref, send_sem=send_sems.at[0], recv_sem=gather_sems.at[step - 1],
            device_id={"fit": source}, device_id_type=MESH,
        ).wait_recv()
    local.wait()
    out.finish()


def fit_sum(part, collective_id):
    F = lax.axis_size("fit")
    piece = (part.shape[0] // F,) + part.shape[1:]
    return pl.pallas_call(
        sum_kernel,
        out_shape=jax.ShapeDtypeStruct(part.shape, part.dtype),
        in_specs=[pl.BlockSpec(memory_space=pltpu.VMEM)],
        out_specs=ANY,
        scratch_shapes=[
            pltpu.VMEM((F - 1,) + piece, part.dtype),
            pltpu.VMEM(piece, part.dtype),
            pltpu.SemaphoreType.DMA((2 * F,)),
            pltpu.SemaphoreType.DMA((F,)),
            pltpu.SemaphoreType.DMA((F,)),
            pltpu.SemaphoreType.DMA,
        ],
        name="fit_sum",
        compiler_params=pltpu.CompilerParams(collective_id=collective_id, has_side_effects=True),
    )(part)


def couple_kernel(block, pair_count, first_turn, row_ref, shift_ref, fock_ref, pick_ref, tiles, inter, base, out, *kept):
    links, size = inter.shape[1], inter.shape[2]
    lane = lax.broadcasted_iota(jnp.int32, (1, LANES), 1)
    first = pl.program_id(0) * block

    def pair(q, carry):
        p = first + q
        halves, sides = [], []
        for k in range(links):
            n = k * pair_count + p
            side = inter[q, k]
            half = jnp.dot(side[:, :size], tiles[row_ref[n]], preferred_element_type=jnp.float32)
            shift = shift_ref[n]
            chosen = jnp.logical_and(lane >= shift, lane < shift + size)
            halves.append((half * jnp.where(chosen, fock_ref[n], 0.0)).astype(jnp.bfloat16))
            sides.append(side)
        coupling = lax.dot_general(
            jnp.concatenate(halves, axis=1), jnp.concatenate(sides, axis=1),
            (((1,), (1,)), ((), ())), preferred_element_type=jnp.float32,
        )
        if first_turn:
            kept[0][q] = coupling
            out[q] = (base[pick_ref[p]] - coupling).astype(out.dtype)
        else:
            out[q] = (base[q] - coupling).astype(out.dtype)
        return carry

    lax.fori_loop(0, block, pair, 0, unroll=4)


def couple(first_turn, rows, shifts, fock, picks, tiles, inter, base):
    pair_count, links, size, _ = inter.shape
    block = 16
    smem = pl.BlockSpec(memory_space=pltpu.SMEM)
    whole = lambda shape: pl.BlockSpec(shape, lambda i: (0, 0, 0), pipeline_mode=pl.Buffered(1))
    by_pair = pl.BlockSpec((block, size, size), lambda i: (i, 0, 0))
    shapes = [jax.ShapeDtypeStruct((pair_count, size, size), jnp.bfloat16)]
    if first_turn:
        shapes.append(jax.ShapeDtypeStruct((pair_count, size, size), jnp.float32))
    return pl.pallas_call(
        functools.partial(couple_kernel, block, pair_count, first_turn),
        grid=(pair_count // block,),
        out_shape=shapes,
        in_specs=[
            smem, smem, smem, smem,
            whole(tiles.shape),
            pl.BlockSpec((block, links, size, LANES), lambda i: (i, 0, 0, 0)),
            whole(base.shape) if first_turn else by_pair,
        ],
        out_specs=[by_pair] * len(shapes),
        name="couple",
        compiler_params=pltpu.CompilerParams(vmem_limit_bytes=VMEM_LIMIT),
    )(rows, shifts, fock, picks, tiles, inter, base)


def on_device(
    orbital_ints,
    occ_energy,
    pair_row,
    pair_col,
    virt_energy,
    amplitudes,
    intersections,
    coupling_fock,
    partner_owner,
    partner_slot,
):
    R, C = lax.axis_size("row"), lax.axis_size("col")
    G = R * C
    size = amplitudes.shape[0]
    pair_count = amplitudes.shape[2]
    occ_block = occ_energy.shape[0]
    pack = LANES // size
    depth = -(-pair_count // pack)
    depth += -depth % 4
    direct = G <= 16

    def packed_tiles(current):
        tiles = jnp.transpose(current.astype(jnp.bfloat16), (2, 0, 1))
        tiles = jnp.pad(tiles, ((0, pack * depth - pair_count), (0, 0), (0, 0)))
        parts = [tiles[t * depth : (t + 1) * depth] for t in range(pack)]
        spare = jnp.zeros((depth, size, LANES - pack * size), jnp.bfloat16)
        return jnp.concatenate(parts + [spare], axis=2)

    packed = packed_tiles(amplitudes)
    if direct:
        energy = jnp.pad(occ_energy[None, :], ((0, 7), (0, LANES - occ_block)))
        tiles, row_ints, col_ints, row_en, col_en = gather(packed, 1, orbital_ints, energy)
        row_energy = row_en[:, 0, :occ_block].reshape(-1)
        col_energy = col_en[:, 0, :occ_block].reshape(-1)
        row_ints = row_ints.reshape((-1,) + orbital_ints.shape[1:])
        col_ints = col_ints.reshape((-1,) + orbital_ints.shape[1:])
    else:
        tiles = lax.all_gather(packed, ("row", "col"), axis=0)
        row_ints = lax.all_gather(orbital_ints, "col", axis=0, tiled=True)
        col_ints = lax.all_gather(orbital_ints, "row", axis=0, tiled=True)
        row_energy = lax.all_gather(occ_energy, "col", axis=0, tiled=True)
        col_energy = lax.all_gather(occ_energy, "row", axis=0, tiled=True)
    seconds = col_ints.shape[0]
    exchange = jnp.einsum(
        "iax,jbx->ijab", row_ints, col_ints, preferred_element_type=jnp.float32
    ).reshape(-1, size, size)
    picks = pair_row * seconds + pair_col
    first_hot = (pair_row[:, None] == jnp.arange(row_energy.shape[0])[None, :])
    second_hot = (pair_col[:, None] == jnp.arange(seconds)[None, :])
    occupied = jnp.sum(jnp.where(first_hot, row_energy[None, :], 0.0), axis=1) + jnp.sum(
        jnp.where(second_hot, col_energy[None, :], 0.0), axis=1
    )
    denominator = virt_energy[:, None, :] + virt_energy[None, :, :] - occupied[None, None, :]
    owners = partner_owner[0].T.reshape(-1)
    slots = partner_slot[0].T.reshape(-1)
    turn = sum((slots >= t * depth).astype(jnp.int32) for t in range(1, pack))
    rows = owners * depth + slots - turn * depth
    shifts = turn * size
    fock = coupling_fock.reshape(-1)
    inter = jnp.transpose(intersections, (3, 2, 0, 1))
    spare = jnp.zeros(inter.shape[:3] + (LANES - pack * size,), inter.dtype)
    inter = jnp.concatenate([inter] * pack + [spare], axis=3)
    current = amplitudes
    residual = amplitudes
    base = exchange
    for step in range(ITERS):
        if step > 0:
            packed = packed_tiles(current)
            if direct:
                (tiles,) = gather(packed, 2)
            else:
                tiles = lax.all_gather(packed, ("row", "col"), axis=0)
        tiles = tiles.reshape(G * depth, size, LANES)
        part, *kept = couple(step == 0, rows, shifts, fock, picks, tiles, inter, base)
        change = fit_sum(jnp.transpose(part, (1, 2, 0)), 3).astype(jnp.float32)
        if step == 0:
            base = kept[0]
            total = change
        else:
            total = total + change
        residual = total + denominator * current
        current = current - residual / denominator
    return (current, residual)


def solution(mesh):
    placed = (
        P(("row", "col"), None, "fit"),
        P(("row", "col")),
        P(("row", "col")),
        P(("row", "col")),
        P(None, ("row", "col")),
        P(None, None, ("row", "col")),
        P(None, None, "fit", ("row", "col")),
        P("fit", ("row", "col")),
        P("fit", ("row", "col"), None),
        P("fit", ("row", "col"), None),
    )
    out = P(None, None, ("row", "col"))
    return jax.shard_map(
        on_device, mesh=mesh, in_specs=placed, out_specs=(out, out), check_vma=False
    )
```

```python
import functools
import math

import jax
import jax.numpy as jnp
from jax import lax
from jax.experimental import pallas as pl
from jax.experimental.pallas import tpu as pltpu
from jax.sharding import PartitionSpec as P

ITERS = 2
LANES = 128
MESH = pl.DeviceIdType.MESH
ANY = pl.BlockSpec(memory_space=pl.ANY)
VMEM_LIMIT = 60 * 1024 * 1024


class Sender:
    def __init__(self, send_sems):
        self.send_sems, self.started = send_sems, []

    def send(self, source, target, recv_sem, device, when=None):
        copy = pltpu.make_async_remote_copy(
            src_ref=source,
            dst_ref=target,
            send_sem=self.send_sems.at[len(self.started)],
            recv_sem=recv_sem,
            device_id=device,
            device_id_type=MESH,
        )
        self.started.append((copy, when))
        guarded(when, copy.start)

    def finish(self):
        for copy, when in self.started:
            guarded(when, copy.wait_send)


def guarded(when, action):
    if when is None:
        action()
    else:
        pl.when(when)(action)


def both(first, second):
    return second if first is None else first if second is None else jnp.logical_and(first, second)


def greet(axes):
    barrier = pltpu.get_barrier_semaphore()
    total = 0
    for axis in axes:
        count = lax.axis_size(axis)
        here = lax.axis_index(axis)
        for step in range(1, count):
            pl.semaphore_signal(
                barrier, inc=1, device_id={axis: lax.rem(here + step, count)}, device_id_type=MESH
            )
            total += 1
    pl.semaphore_wait(barrier, total)


def gather_kernel(sizes, with_ints, *refs):
    if with_ints:
        own, ints, energy, tiles, row_ints, col_ints, row_en, col_en = refs[:8]
        send_sems, recv_sems, part_sems, int_sems, local_sems = refs[8:]
    else:
        own, tiles, send_sems, recv_sems, part_sems, local_sems = refs
    R, C = lax.axis_size("row"), lax.axis_size("col")
    r, c, f = lax.axis_index("row"), lax.axis_index("col"), lax.axis_index("fit")
    partner = {"fit": f + 1 - 2 * lax.rem(f, 2)}
    half = sum(sizes)
    count = len(sizes) // 2
    lengthwise, crosswise = range(count), range(count, 2 * count)
    mine = lax.rem(f, 2) * half
    theirs = half - mine
    me = r * C + c
    greet(("row", "col", "fit"))
    out = Sender(send_sems)
    offsets = [sum(sizes[:piece]) for piece in range(2 * count)]

    def place(piece, group, base=mine):
        return tiles.at[group, pl.ds(base + offsets[piece], sizes[piece])]

    def await_copy(piece, group, sem, base=mine, when=None):
        ref = place(piece, group, base)
        copy = pltpu.make_async_remote_copy(
            src_ref=ref, dst_ref=ref, send_sem=send_sems.at[0], recv_sem=sem,
            device_id=partner, device_id_type=MESH,
        )
        guarded(when, copy.wait_recv)

    def along(piece, group, step, when=None, source=None):
        inside = c + 1 < C if step > 0 else c > 0
        out.send(
            place(piece, group) if source is None else source, place(piece, group),
            recv_sems.at[piece, group], {"col": c + step}, both(when, inside),
        )

    def across(piece, group, when=None, source=None):
        for step in range(1, R):
            out.send(
                place(piece, group) if source is None else source, place(piece, group),
                recv_sems.at[piece, group], {"row": lax.rem(r + step, R)}, when,
            )

    def beside(piece, group, when=None):
        out.send(place(piece, group), place(piece, group), part_sems.at[piece, group], partner, when)

    def own_piece(piece):
        return own.at[pl.ds(mine + offsets[piece], sizes[piece])]

    for long_piece, cross_piece in zip(lengthwise, crosswise):
        across(cross_piece, me, source=own_piece(cross_piece))
        for step in (1, -1):
            along(long_piece, me, step, source=own_piece(long_piece))
    if with_ints:
        def int_wait(target, sem, when=None):
            copy = pltpu.make_async_remote_copy(
                src_ref=target, dst_ref=target, send_sem=send_sems.at[0], recv_sem=sem,
                device_id=partner, device_id_type=MESH,
            )
            guarded(when, copy.wait_recv)

        for step in (1, -1):
            inside = c + 1 < C if step > 0 else c > 0
            out.send(ints, row_ints.at[c], int_sems.at[0, c], {"col": c + step}, inside)
        for step in range(1, R):
            to = {"row": lax.rem(r + step, R)}
            out.send(ints, col_ints.at[r], int_sems.at[1, r], to)
            out.send(energy, col_en.at[r], int_sems.at[3, r], to)
        for step in range(1, C):
            to = {"col": lax.rem(c + step, C)}
            out.send(energy, row_en.at[c], int_sems.at[2, c], to)
    for long_piece, cross_piece in zip(lengthwise, crosswise):
        for step in (1, -1):
            along(cross_piece, me, step, source=own_piece(cross_piece))
        across(long_piece, me, source=own_piece(long_piece))
    local = [pltpu.make_async_copy(own, tiles.at[me], local_sems.at[0])]
    if with_ints:
        local += [
            pltpu.make_async_copy(ints, row_ints.at[c], local_sems.at[1]),
            pltpu.make_async_copy(ints, col_ints.at[r], local_sems.at[2]),
            pltpu.make_async_copy(energy, row_en.at[c], local_sems.at[3]),
            pltpu.make_async_copy(energy, col_en.at[r], local_sems.at[4]),
        ]
    for copy in local:
        copy.start()
    for piece in crosswise:
        for other in range(1, R):
            group = lax.rem(r + other, R) * C + c
            await_copy(piece, group, recv_sems.at[piece, group])
            for step in (1, -1):
                along(piece, group, step)
            beside(piece, group)
    for distance in range(1, C):
        for long_piece, cross_piece in zip(lengthwise, crosswise):
            for step in (1, -1):
                source = c - step * distance
                there = jnp.logical_and(source >= 0, source < C)
                column = jnp.clip(source, 0, C - 1)
                group = r * C + column
                await_copy(long_piece, group, recv_sems.at[long_piece, group], when=there)
                if distance < C - 1:
                    along(long_piece, group, step, there)
                across(long_piece, group, there)
                beside(long_piece, group, there)
                for other in range(R):
                    group = lax.rem(r + other, R) * C + column
                    await_copy(cross_piece, group, recv_sems.at[cross_piece, group], when=there)
                    if distance < C - 1:
                        along(cross_piece, group, step, there)
                    beside(cross_piece, group, there)
        for step in (1, -1):
            source = c - step * distance
            there = jnp.logical_and(source >= 0, source < C)
            column = jnp.clip(source, 0, C - 1)
            if with_ints:
                int_wait(row_ints.at[column], int_sems.at[0, column], there)
                if distance < C - 1:
                    inside = c + 1 < C if step > 0 else c > 0
                    out.send(
                        row_ints.at[column], row_ints.at[column], int_sems.at[0, column],
                        {"col": c + step}, both(there, inside),
                    )
    for other in range(1, R):
        for turn in range(C):
            group = lax.rem(r + other, R) * C + lax.rem(c + turn, C)
            for piece in lengthwise:
                await_copy(piece, group, recv_sems.at[piece, group])
                beside(piece, group)
    if with_ints:
        for step in range(1, R):
            row = lax.rem(r + step, R)
            int_wait(col_ints.at[row], int_sems.at[1, row])
            int_wait(col_en.at[row], int_sems.at[3, row])
        for step in range(1, C):
            column = lax.rem(c + step, C)
            int_wait(row_en.at[column], int_sems.at[2, column])
    for step in range(1, R * C):
        group = lax.rem(me + step, R * C)
        for piece in range(2 * count):
            await_copy(piece, group, part_sems.at[piece, group], base=theirs)
    for copy in local:
        copy.wait()
    out.finish()


def gather(packed, collective_id, ints=None, energy=None):
    R, C = lax.axis_size("row"), lax.axis_size("col")
    G = R * C
    with_ints = ints is not None
    half = packed.shape[0] // 2
    first = (half * 3 + 4) // 5
    count = max(1, min(3, half - first))
    sizes = tuple(len(range(i, total, count)) for total in (first, half - first) for i in range(count))
    shapes = [jax.ShapeDtypeStruct((G,) + packed.shape, packed.dtype)]
    operands = [packed]
    if with_ints:
        operands += [ints, energy]
        shapes += [
            jax.ShapeDtypeStruct((C,) + ints.shape, ints.dtype),
            jax.ShapeDtypeStruct((R,) + ints.shape, ints.dtype),
            jax.ShapeDtypeStruct((C,) + energy.shape, energy.dtype),
            jax.ShapeDtypeStruct((R,) + energy.shape, energy.dtype),
        ]
    scratch = [
        pltpu.SemaphoreType.DMA((8 * len(sizes) * G + 32,)),
        pltpu.SemaphoreType.DMA((len(sizes), G)),
        pltpu.SemaphoreType.DMA((len(sizes), G)),
    ]
    if with_ints:
        scratch.append(pltpu.SemaphoreType.DMA((4, max(R, C))))
    scratch.append(pltpu.SemaphoreType.DMA((5,)))
    return pl.pallas_call(
        functools.partial(gather_kernel, sizes, with_ints),
        out_shape=shapes,
        in_specs=[ANY] * len(operands),
        out_specs=[ANY] * len(shapes),
        scratch_shapes=scratch,
        name="gather_ints" if with_ints else "gather_tiles",
        compiler_params=pltpu.CompilerParams(
            collective_id=collective_id, has_side_effects=True, vmem_limit_bytes=VMEM_LIMIT
        ),
    )(*operands)


def sum_kernel(part, total, inbox, result, send_sems, recv_sems, gather_sems, local_sem):
    F = lax.axis_size("fit")
    f = lax.axis_index("fit")
    rows = part.shape[0] // F
    greet(("fit",))
    out = Sender(send_sems)
    for step in range(1, F):
        to = lax.rem(f + step, F)
        out.send(
            part.at[pl.ds(to * rows, rows)], inbox.at[step - 1], recv_sems.at[step - 1], {"fit": to}
        )
    value = part[pl.ds(f * rows, rows)].astype(jnp.float32)
    for step in range(1, F):
        pltpu.make_async_remote_copy(
            src_ref=inbox.at[step - 1], dst_ref=inbox.at[step - 1], send_sem=send_sems.at[0],
            recv_sem=recv_sems.at[step - 1], device_id={"fit": lax.rem(f + step, F)},
            device_id_type=MESH,
        ).wait_recv()
        value = value + inbox[step - 1].astype(jnp.float32)
    result[...] = value.astype(result.dtype)
    target = total.at[pl.ds(f * rows, rows)]
    for step in range(1, F):
        out.send(result, target, gather_sems.at[step - 1], {"fit": lax.rem(f + step, F)})
    local = pltpu.make_async_copy(result, target, local_sem)
    local.start()
    for step in range(1, F):
        source = lax.rem(f + F - step, F)
        ref = total.at[pl.ds(source * rows, rows)]
        pltpu.make_async_remote_copy(
            src_ref=ref, dst_ref=ref, send_sem=send_sems.at[0], recv_sem=gather_sems.at[step - 1],
            device_id={"fit": source}, device_id_type=MESH,
        ).wait_recv()
    local.wait()
    out.finish()


def fit_sum(part, collective_id):
    F = lax.axis_size("fit")
    piece = (part.shape[0] // F,) + part.shape[1:]
    return pl.pallas_call(
        sum_kernel,
        out_shape=jax.ShapeDtypeStruct(part.shape, part.dtype),
        in_specs=[pl.BlockSpec(memory_space=pltpu.VMEM)],
        out_specs=ANY,
        scratch_shapes=[
            pltpu.VMEM((F - 1,) + piece, part.dtype),
            pltpu.VMEM(piece, part.dtype),
            pltpu.SemaphoreType.DMA((2 * F,)),
            pltpu.SemaphoreType.DMA((F,)),
            pltpu.SemaphoreType.DMA((F,)),
            pltpu.SemaphoreType.DMA,
        ],
        name="fit_sum",
        compiler_params=pltpu.CompilerParams(collective_id=collective_id, has_side_effects=True),
    )(part)


def couple_kernel(block, pair_count, first_turn, row_ref, shift_ref, fock_ref, pick_ref, tiles, inter, base, out, *kept):
    links, size = inter.shape[1], inter.shape[2]
    first = pl.program_id(0) * block
    halves, results = [], []
    for q in range(block):
        for k in range(links):
            n = k * pair_count + first + q
            tile = pltpu.roll(tiles[row_ref[n]], shift_ref[n], 1)[:, :size]
            halves.append(jnp.dot(inter[q, k], tile, preferred_element_type=jnp.float32))
    for q in range(block):
        for k in range(links):
            scale = fock_ref[k * pair_count + first + q]
            halves[q * links + k] = (halves[q * links + k] * scale).astype(jnp.bfloat16)
    for q in range(block):
        results.append(
            sum(
                lax.dot_general(
                    halves[q * links + k], inter[q, k], (((1,), (1,)), ((), ())),
                    preferred_element_type=jnp.float32,
                )
                for k in range(links)
            )
        )
    for q in range(block):
        if first_turn:
            kept[0][q] = results[q]
            out[q] = (base[pick_ref[first + q]] - results[q]).astype(out.dtype)
        else:
            out[q] = (base[q] - results[q]).astype(out.dtype)


def couple(first_turn, rows, shifts, fock, picks, tiles, inter, base):
    pair_count, links, size, _ = inter.shape
    block = math.gcd(pair_count, 16)
    smem = pl.BlockSpec(memory_space=pltpu.SMEM)
    whole = lambda shape: pl.BlockSpec(shape, lambda i: (0, 0, 0), pipeline_mode=pl.Buffered(1))
    by_pair = pl.BlockSpec((block, size, size), lambda i: (i, 0, 0))
    shapes = [jax.ShapeDtypeStruct((pair_count, size, size), jnp.bfloat16)]
    if first_turn:
        shapes.append(jax.ShapeDtypeStruct((pair_count, size, size), jnp.float32))
    return pl.pallas_call(
        functools.partial(couple_kernel, block, pair_count, first_turn),
        grid=(pair_count // block,),
        out_shape=shapes,
        in_specs=[
            smem, smem, smem, smem,
            whole(tiles.shape),
            pl.BlockSpec((block, links, size, size), lambda i: (i, 0, 0, 0)),
            whole(base.shape) if first_turn else by_pair,
        ],
        out_specs=[by_pair] * len(shapes),
        name="couple",
        compiler_params=pltpu.CompilerParams(vmem_limit_bytes=VMEM_LIMIT),
    )(rows, shifts, fock, picks, tiles, inter, base)


def on_device(
    orbital_ints,
    occ_energy,
    pair_row,
    pair_col,
    virt_energy,
    amplitudes,
    intersections,
    coupling_fock,
    partner_owner,
    partner_slot,
):
    R, C = lax.axis_size("row"), lax.axis_size("col")
    G = R * C
    size = amplitudes.shape[0]
    pair_count = amplitudes.shape[2]
    occ_block = occ_energy.shape[0]
    pack = LANES // size
    depth = -(-pair_count // pack)
    depth += -depth % 4
    direct = G <= 16

    def packed_tiles(current):
        tiles = jnp.transpose(current.astype(jnp.bfloat16), (2, 0, 1))
        tiles = jnp.pad(tiles, ((0, pack * depth - pair_count), (0, 0), (0, 0)))
        parts = [tiles[t * depth : (t + 1) * depth] for t in range(pack)]
        spare = jnp.zeros((depth, size, LANES - pack * size), jnp.bfloat16)
        return jnp.concatenate(parts + [spare], axis=2)

    packed = packed_tiles(amplitudes)
    if direct:
        energy = jnp.pad(occ_energy[None, :], ((0, 7), (0, LANES - occ_block)))
        tiles, row_ints, col_ints, row_en, col_en = gather(packed, 1, orbital_ints, energy)
        row_energy = row_en[:, 0, :occ_block].reshape(-1)
        col_energy = col_en[:, 0, :occ_block].reshape(-1)
        row_ints = row_ints.reshape((-1,) + orbital_ints.shape[1:])
        col_ints = col_ints.reshape((-1,) + orbital_ints.shape[1:])
    else:
        tiles = lax.all_gather(packed, ("row", "col"), axis=0)
        row_ints = lax.all_gather(orbital_ints, "col", axis=0, tiled=True)
        col_ints = lax.all_gather(orbital_ints, "row", axis=0, tiled=True)
        row_energy = lax.all_gather(occ_energy, "col", axis=0, tiled=True)
        col_energy = lax.all_gather(occ_energy, "row", axis=0, tiled=True)
    seconds = col_ints.shape[0]
    exchange = jnp.einsum(
        "iax,jbx->ijab", row_ints, col_ints, preferred_element_type=jnp.float32
    ).reshape(-1, size, size)
    picks = pair_row * seconds + pair_col
    first_hot = (pair_row[:, None] == jnp.arange(row_energy.shape[0])[None, :])
    second_hot = (pair_col[:, None] == jnp.arange(seconds)[None, :])
    occupied = jnp.sum(jnp.where(first_hot, row_energy[None, :], 0.0), axis=1) + jnp.sum(
        jnp.where(second_hot, col_energy[None, :], 0.0), axis=1
    )
    denominator = virt_energy[:, None, :] + virt_energy[None, :, :] - occupied[None, None, :]
    owners = partner_owner[0].T.reshape(-1)
    slots = partner_slot[0].T.reshape(-1)
    turn = sum((slots >= t * depth).astype(jnp.int32) for t in range(1, pack))
    rows = owners * depth + slots - turn * depth
    shifts = jnp.where(turn == 0, 0, LANES - turn * size)
    fock = coupling_fock.reshape(-1)
    inter = jnp.transpose(intersections, (3, 2, 0, 1))
    current = amplitudes
    residual = amplitudes
    base = exchange
    for step in range(ITERS):
        if step > 0:
            packed = packed_tiles(current)
            if direct:
                (tiles,) = gather(packed, 2)
            else:
                tiles = lax.all_gather(packed, ("row", "col"), axis=0)
        tiles = tiles.reshape(G * depth, size, LANES)
        part, *kept = couple(step == 0, rows, shifts, fock, picks, tiles, inter, base)
        change = fit_sum(jnp.transpose(part, (1, 2, 0)), 3).astype(jnp.float32)
        if step == 0:
            base = kept[0]
            total = change
        else:
            total = total + change
        residual = total + denominator * current
        current = current - residual / denominator
    return (current, residual)


def solution(mesh):
    placed = (
        P(("row", "col"), None, "fit"),
        P(("row", "col")),
        P(("row", "col")),
        P(("row", "col")),
        P(None, ("row", "col")),
        P(None, None, ("row", "col")),
        P(None, None, "fit", ("row", "col")),
        P("fit", ("row", "col")),
        P("fit", ("row", "col"), None),
        P("fit", ("row", "col"), None),
    )
    out = P(None, None, ("row", "col"))
    return jax.shard_map(
        on_device, mesh=mesh, in_specs=placed, out_specs=(out, out), check_vma=False
    )
```

```python
import functools
import math

import jax
import jax.numpy as jnp
from jax import lax
from jax.experimental import pallas as pl
from jax.experimental.pallas import tpu as pltpu
from jax.sharding import PartitionSpec as P

ITERS = 2
LANES = 128
MESH = pl.DeviceIdType.MESH
ANY = pl.BlockSpec(memory_space=pl.ANY)
VMEM_LIMIT = 60 * 1024 * 1024


class Sender:
    def __init__(self, send_sems):
        self.send_sems, self.started = send_sems, []

    def send(self, source, target, recv_sem, device, when=None):
        copy = pltpu.make_async_remote_copy(
            src_ref=source,
            dst_ref=target,
            send_sem=self.send_sems.at[len(self.started)],
            recv_sem=recv_sem,
            device_id=device,
            device_id_type=MESH,
        )
        self.started.append((copy, when))
        guarded(when, copy.start)

    def finish(self):
        for copy, when in self.started:
            guarded(when, copy.wait_send)


def guarded(when, action):
    if when is None:
        action()
    else:
        pl.when(when)(action)


def both(first, second):
    return second if first is None else first if second is None else jnp.logical_and(first, second)


def greet(axes):
    barrier = pltpu.get_barrier_semaphore()
    total = 0
    for axis in axes:
        count = lax.axis_size(axis)
        here = lax.axis_index(axis)
        for step in range(1, count):
            pl.semaphore_signal(
                barrier, inc=1, device_id={axis: lax.rem(here + step, count)}, device_id_type=MESH
            )
            total += 1
    pl.semaphore_wait(barrier, total)


def gather_kernel(sizes, with_ints, *refs):
    if with_ints:
        own, ints, energy, tiles, row_ints, col_ints, row_en, col_en = refs[:8]
        send_sems, recv_sems, part_sems, int_sems, local_sems = refs[8:]
    else:
        own, tiles, send_sems, recv_sems, part_sems, local_sems = refs
    R, C = lax.axis_size("row"), lax.axis_size("col")
    r, c, f = lax.axis_index("row"), lax.axis_index("col"), lax.axis_index("fit")
    partner = {"fit": f + 1 - 2 * lax.rem(f, 2)}
    half = sum(sizes)
    count = len(sizes)
    pieces = range(count)
    mine = lax.rem(f, 2) * half
    theirs = half - mine
    me = r * C + c
    greet(("row", "col", "fit"))
    out = Sender(send_sems)
    offsets = [sum(sizes[:piece]) for piece in pieces]

    def place(piece, group, base=mine):
        return tiles.at[group, pl.ds(base + offsets[piece], sizes[piece])]

    def await_copy(piece, group, sem, base=mine, when=None):
        ref = place(piece, group, base)
        copy = pltpu.make_async_remote_copy(
            src_ref=ref, dst_ref=ref, send_sem=send_sems.at[0], recv_sem=sem,
            device_id=partner, device_id_type=MESH,
        )
        guarded(when, copy.wait_recv)

    def along(piece, group, step, when=None, source=None):
        inside = c + 1 < C if step > 0 else c > 0
        out.send(
            place(piece, group) if source is None else source, place(piece, group),
            recv_sems.at[piece, group], {"col": c + step}, both(when, inside),
        )

    def across(piece, group, when=None, source=None):
        for step in range(1, R):
            out.send(
                place(piece, group) if source is None else source, place(piece, group),
                recv_sems.at[piece, group], {"row": lax.rem(r + step, R)}, when,
            )

    def beside(piece, group, when=None):
        out.send(place(piece, group), place(piece, group), part_sems.at[piece, group], partner, when)

    def own_piece(piece):
        return own.at[pl.ds(mine + offsets[piece], sizes[piece])]

    for piece in pieces:
        for step in (1, -1):
            along(piece, me, step, source=own_piece(piece))
        across(piece, me, source=own_piece(piece))
    if with_ints:
        def int_wait(target, sem, when=None):
            copy = pltpu.make_async_remote_copy(
                src_ref=target, dst_ref=target, send_sem=send_sems.at[0], recv_sem=sem,
                device_id=partner, device_id_type=MESH,
            )
            guarded(when, copy.wait_recv)

        for step in (1, -1):
            inside = c + 1 < C if step > 0 else c > 0
            out.send(ints, row_ints.at[c], int_sems.at[0, c], {"col": c + step}, inside)
        for step in range(1, R):
            to = {"row": lax.rem(r + step, R)}
            out.send(ints, col_ints.at[r], int_sems.at[1, r], to)
            out.send(energy, col_en.at[r], int_sems.at[3, r], to)
        for step in range(1, C):
            to = {"col": lax.rem(c + step, C)}
            out.send(energy, row_en.at[c], int_sems.at[2, c], to)
    local = [pltpu.make_async_copy(own, tiles.at[me], local_sems.at[0])]
    if with_ints:
        local += [
            pltpu.make_async_copy(ints, row_ints.at[c], local_sems.at[1]),
            pltpu.make_async_copy(ints, col_ints.at[r], local_sems.at[2]),
            pltpu.make_async_copy(energy, row_en.at[c], local_sems.at[3]),
            pltpu.make_async_copy(energy, col_en.at[r], local_sems.at[4]),
        ]
    for copy in local:
        copy.start()
    events = []

    def behind(step, distance):
        source = c - step * distance
        there = jnp.logical_and(source >= 0, source < C)
        return jnp.clip(source, 0, C - 1), there

    def arrival(piece, step, distance):
        column, there = behind(step, distance)
        group = r * C + column
        await_copy(piece, group, recv_sems.at[piece, group], when=there)
        if distance < C - 1:
            along(piece, group, step, there)
        across(piece, group, there)
        beside(piece, group, there)

    def crossed(piece, other, step, distance):
        column, there = behind(step, distance)
        group = lax.rem(r + other, R) * C + column
        await_copy(piece, group, recv_sems.at[piece, group], when=there)
        beside(piece, group, there)

    def int_arrival(step, distance):
        column, there = behind(step, distance)
        int_wait(row_ints.at[column], int_sems.at[0, column], there)
        if distance < C - 1:
            inside = c + 1 < C if step > 0 else c > 0
            out.send(
                row_ints.at[column], row_ints.at[column], int_sems.at[0, column],
                {"col": c + step}, both(there, inside),
            )

    for piece in pieces:
        for other in range(1, R):
            events.append((1.5, piece, functools.partial(crossed, piece, other, 1, 0)))
        for distance in range(1, C):
            for step in (1, -1):
                events.append((distance, piece, functools.partial(arrival, piece, step, distance)))
                for other in range(1, R):
                    events.append((
                        distance + 1.5, piece, functools.partial(crossed, piece, other, step, distance)
                    ))
    if with_ints:
        for distance in range(1, C):
            for step in (1, -1):
                events.append((distance, count, functools.partial(int_arrival, step, distance)))
    for _, _, event in sorted(events, key=lambda entry: entry[:2]):
        event()
    if with_ints:
        for step in range(1, R):
            row = lax.rem(r + step, R)
            int_wait(col_ints.at[row], int_sems.at[1, row])
            int_wait(col_en.at[row], int_sems.at[3, row])
        for step in range(1, C):
            column = lax.rem(c + step, C)
            int_wait(row_en.at[column], int_sems.at[2, column])
    for step in range(1, R * C):
        group = lax.rem(me + step, R * C)
        for piece in pieces:
            await_copy(piece, group, part_sems.at[piece, group], base=theirs)
    for copy in local:
        copy.wait()
    out.finish()


def gather(packed, collective_id, ints=None, energy=None):
    R, C = lax.axis_size("row"), lax.axis_size("col")
    G = R * C
    with_ints = ints is not None
    half = packed.shape[0] // 2
    count = min(2, half)
    sizes = tuple(len(range(i, half, count)) for i in range(count))
    shapes = [jax.ShapeDtypeStruct((G,) + packed.shape, packed.dtype)]
    operands = [packed]
    if with_ints:
        operands += [ints, energy]
        shapes += [
            jax.ShapeDtypeStruct((C,) + ints.shape, ints.dtype),
            jax.ShapeDtypeStruct((R,) + ints.shape, ints.dtype),
            jax.ShapeDtypeStruct((C,) + energy.shape, energy.dtype),
            jax.ShapeDtypeStruct((R,) + energy.shape, energy.dtype),
        ]
    scratch = [
        pltpu.SemaphoreType.DMA((8 * len(sizes) * G + 32,)),
        pltpu.SemaphoreType.DMA((len(sizes), G)),
        pltpu.SemaphoreType.DMA((len(sizes), G)),
    ]
    if with_ints:
        scratch.append(pltpu.SemaphoreType.DMA((4, max(R, C))))
    scratch.append(pltpu.SemaphoreType.DMA((5,)))
    return pl.pallas_call(
        functools.partial(gather_kernel, sizes, with_ints),
        out_shape=shapes,
        in_specs=[ANY] * len(operands),
        out_specs=[ANY] * len(shapes),
        scratch_shapes=scratch,
        name="gather_ints" if with_ints else "gather_tiles",
        compiler_params=pltpu.CompilerParams(
            collective_id=collective_id, has_side_effects=True, vmem_limit_bytes=VMEM_LIMIT
        ),
    )(*operands)


def sum_kernel(part, total, inbox, result, send_sems, recv_sems, gather_sems, local_sem):
    F = lax.axis_size("fit")
    f = lax.axis_index("fit")
    rows = part.shape[0] // F
    greet(("fit",))
    out = Sender(send_sems)
    for step in range(1, F):
        to = lax.rem(f + step, F)
        out.send(
            part.at[pl.ds(to * rows, rows)], inbox.at[step - 1], recv_sems.at[step - 1], {"fit": to}
        )
    value = part[pl.ds(f * rows, rows)].astype(jnp.float32)
    for step in range(1, F):
        pltpu.make_async_remote_copy(
            src_ref=inbox.at[step - 1], dst_ref=inbox.at[step - 1], send_sem=send_sems.at[0],
            recv_sem=recv_sems.at[step - 1], device_id={"fit": lax.rem(f + step, F)},
            device_id_type=MESH,
        ).wait_recv()
        value = value + inbox[step - 1].astype(jnp.float32)
    result[...] = value.astype(result.dtype)
    target = total.at[pl.ds(f * rows, rows)]
    for step in range(1, F):
        out.send(result, target, gather_sems.at[step - 1], {"fit": lax.rem(f + step, F)})
    local = pltpu.make_async_copy(result, target, local_sem)
    local.start()
    for step in range(1, F):
        source = lax.rem(f + F - step, F)
        ref = total.at[pl.ds(source * rows, rows)]
        pltpu.make_async_remote_copy(
            src_ref=ref, dst_ref=ref, send_sem=send_sems.at[0], recv_sem=gather_sems.at[step - 1],
            device_id={"fit": source}, device_id_type=MESH,
        ).wait_recv()
    local.wait()
    out.finish()


def fit_sum(part, collective_id):
    F = lax.axis_size("fit")
    piece = (part.shape[0] // F,) + part.shape[1:]
    return pl.pallas_call(
        sum_kernel,
        out_shape=jax.ShapeDtypeStruct(part.shape, part.dtype),
        in_specs=[pl.BlockSpec(memory_space=pltpu.VMEM)],
        out_specs=ANY,
        scratch_shapes=[
            pltpu.VMEM((F - 1,) + piece, part.dtype),
            pltpu.VMEM(piece, part.dtype),
            pltpu.SemaphoreType.DMA((2 * F,)),
            pltpu.SemaphoreType.DMA((F,)),
            pltpu.SemaphoreType.DMA((F,)),
            pltpu.SemaphoreType.DMA,
        ],
        name="fit_sum",
        compiler_params=pltpu.CompilerParams(collective_id=collective_id, has_side_effects=True),
    )(part)


def couple_kernel(block, pair_count, first_turn, row_ref, shift_ref, fock_ref, pick_ref, tiles, inter, base, out, *kept):
    links, size = inter.shape[1], inter.shape[2]
    first = pl.program_id(0) * block
    halves, results = [], []
    for q in range(block):
        for k in range(links):
            n = k * pair_count + first + q
            tile = pltpu.roll(tiles[row_ref[n]], shift_ref[n], 1)[:, :size]
            halves.append(jnp.dot(inter[q, k], tile, preferred_element_type=jnp.float32))
    for q in range(block):
        for k in range(links):
            scale = fock_ref[k * pair_count + first + q]
            halves[q * links + k] = (halves[q * links + k] * scale).astype(jnp.bfloat16)
    for q in range(block):
        results.append(
            sum(
                lax.dot_general(
                    halves[q * links + k], inter[q, k], (((1,), (1,)), ((), ())),
                    preferred_element_type=jnp.float32,
                )
                for k in range(links)
            )
        )
    for q in range(block):
        if first_turn:
            kept[0][q] = results[q]
            out[q] = (base[pick_ref[first + q]] - results[q]).astype(out.dtype)
        else:
            out[q] = (base[q] - results[q]).astype(out.dtype)


def couple(first_turn, rows, shifts, fock, picks, tiles, inter, base):
    pair_count, links, size, _ = inter.shape
    block = math.gcd(pair_count, 16)
    smem = pl.BlockSpec(memory_space=pltpu.SMEM)
    whole = lambda shape: pl.BlockSpec(shape, lambda i: (0, 0, 0), pipeline_mode=pl.Buffered(1))
    by_pair = pl.BlockSpec((block, size, size), lambda i: (i, 0, 0))
    shapes = [jax.ShapeDtypeStruct((pair_count, size, size), jnp.bfloat16)]
    if first_turn:
        shapes.append(jax.ShapeDtypeStruct((pair_count, size, size), jnp.float32))
    return pl.pallas_call(
        functools.partial(couple_kernel, block, pair_count, first_turn),
        grid=(pair_count // block,),
        out_shape=shapes,
        in_specs=[
            smem, smem, smem, smem,
            whole(tiles.shape),
            pl.BlockSpec((block, links, size, size), lambda i: (i, 0, 0, 0)),
            whole(base.shape) if first_turn else by_pair,
        ],
        out_specs=[by_pair] * len(shapes),
        name="couple",
        compiler_params=pltpu.CompilerParams(vmem_limit_bytes=VMEM_LIMIT),
    )(rows, shifts, fock, picks, tiles, inter, base)


def on_device(
    orbital_ints,
    occ_energy,
    pair_row,
    pair_col,
    virt_energy,
    amplitudes,
    intersections,
    coupling_fock,
    partner_owner,
    partner_slot,
):
    R, C = lax.axis_size("row"), lax.axis_size("col")
    G = R * C
    size = amplitudes.shape[0]
    pair_count = amplitudes.shape[2]
    occ_block = occ_energy.shape[0]
    pack = LANES // size
    depth = -(-pair_count // pack)
    depth += -depth % 4
    direct = G <= 16

    def packed_tiles(current):
        tiles = jnp.transpose(current.astype(jnp.bfloat16), (2, 0, 1))
        tiles = jnp.pad(tiles, ((0, pack * depth - pair_count), (0, 0), (0, 0)))
        parts = [tiles[t * depth : (t + 1) * depth] for t in range(pack)]
        spare = jnp.zeros((depth, size, LANES - pack * size), jnp.bfloat16)
        return jnp.concatenate(parts + [spare], axis=2)

    packed = packed_tiles(amplitudes)
    if direct:
        energy = jnp.pad(occ_energy[None, :], ((0, 7), (0, LANES - occ_block)))
        tiles, row_ints, col_ints, row_en, col_en = gather(packed, 1, orbital_ints, energy)
        row_energy = row_en[:, 0, :occ_block].reshape(-1)
        col_energy = col_en[:, 0, :occ_block].reshape(-1)
        row_ints = row_ints.reshape((-1,) + orbital_ints.shape[1:])
        col_ints = col_ints.reshape((-1,) + orbital_ints.shape[1:])
    else:
        tiles = lax.all_gather(packed, ("row", "col"), axis=0)
        row_ints = lax.all_gather(orbital_ints, "col", axis=0, tiled=True)
        col_ints = lax.all_gather(orbital_ints, "row", axis=0, tiled=True)
        row_energy = lax.all_gather(occ_energy, "col", axis=0, tiled=True)
        col_energy = lax.all_gather(occ_energy, "row", axis=0, tiled=True)
    seconds = col_ints.shape[0]
    exchange = jnp.einsum(
        "iax,jbx->ijab", row_ints, col_ints, preferred_element_type=jnp.float32
    ).reshape(-1, size, size)
    picks = pair_row * seconds + pair_col
    first_hot = (pair_row[:, None] == jnp.arange(row_energy.shape[0])[None, :])
    second_hot = (pair_col[:, None] == jnp.arange(seconds)[None, :])
    occupied = jnp.sum(jnp.where(first_hot, row_energy[None, :], 0.0), axis=1) + jnp.sum(
        jnp.where(second_hot, col_energy[None, :], 0.0), axis=1
    )
    denominator = virt_energy[:, None, :] + virt_energy[None, :, :] - occupied[None, None, :]
    owners = partner_owner[0].T.reshape(-1)
    slots = partner_slot[0].T.reshape(-1)
    turn = sum((slots >= t * depth).astype(jnp.int32) for t in range(1, pack))
    rows = owners * depth + slots - turn * depth
    shifts = jnp.where(turn == 0, 0, LANES - turn * size)
    fock = coupling_fock.reshape(-1)
    inter = jnp.transpose(intersections, (3, 2, 0, 1))
    current = amplitudes
    residual = amplitudes
    base = exchange
    for step in range(ITERS):
        if step > 0:
            packed = packed_tiles(current)
            if direct:
                (tiles,) = gather(packed, 2)
            else:
                tiles = lax.all_gather(packed, ("row", "col"), axis=0)
        tiles = tiles.reshape(G * depth, size, LANES)
        part, *kept = couple(step == 0, rows, shifts, fock, picks, tiles, inter, base)
        change = fit_sum(jnp.transpose(part, (1, 2, 0)), 3).astype(jnp.float32)
        if step == 0:
            base = kept[0]
            total = change
        else:
            total = total + change
        residual = total + denominator * current
        current = current - residual / denominator
    return (current, residual)


def solution(mesh):
    placed = (
        P(("row", "col"), None, "fit"),
        P(("row", "col")),
        P(("row", "col")),
        P(("row", "col")),
        P(None, ("row", "col")),
        P(None, None, ("row", "col")),
        P(None, None, "fit", ("row", "col")),
        P("fit", ("row", "col")),
        P("fit", ("row", "col"), None),
        P("fit", ("row", "col"), None),
    )
    out = P(None, None, ("row", "col"))
    return jax.shard_map(
        on_device, mesh=mesh, in_specs=placed, out_specs=(out, out), check_vma=False
    )
```

```python
import functools
import math

import jax
import jax.numpy as jnp
from jax import lax
from jax.experimental import pallas as pl
from jax.experimental.pallas import tpu as pltpu
from jax.sharding import PartitionSpec as P

ITERS = 2
LANES = 128
MESH = pl.DeviceIdType.MESH
ANY = pl.BlockSpec(memory_space=pl.ANY)
VMEM_LIMIT = 60 * 1024 * 1024


class Sender:
    def __init__(self, send_sems):
        self.send_sems, self.started = send_sems, []

    def send(self, source, target, recv_sem, device, when=None):
        copy = pltpu.make_async_remote_copy(
            src_ref=source,
            dst_ref=target,
            send_sem=self.send_sems.at[len(self.started)],
            recv_sem=recv_sem,
            device_id=device,
            device_id_type=MESH,
        )
        self.started.append((copy, when))
        guarded(when, copy.start)

    def finish(self):
        for copy, when in self.started:
            guarded(when, copy.wait_send)


def guarded(when, action):
    if when is None:
        action()
    else:
        pl.when(when)(action)


def both(first, second):
    return second if first is None else first if second is None else jnp.logical_and(first, second)


def greet(axes):
    barrier = pltpu.get_barrier_semaphore()
    total = 0
    for axis in axes:
        count = lax.axis_size(axis)
        here = lax.axis_index(axis)
        for step in range(1, count):
            pl.semaphore_signal(
                barrier, inc=1, device_id={axis: lax.rem(here + step, count)}, device_id_type=MESH
            )
            total += 1
    pl.semaphore_wait(barrier, total)


def gather_kernel(sizes, with_ints, *refs):
    if with_ints:
        own, ints, energy, tiles, row_ints, col_ints, row_en, col_en = refs[:8]
        send_sems, recv_sems, part_sems, int_sems, local_sems = refs[8:]
    else:
        own, tiles, send_sems, recv_sems, part_sems, local_sems = refs
    R, C = lax.axis_size("row"), lax.axis_size("col")
    r, c, f = lax.axis_index("row"), lax.axis_index("col"), lax.axis_index("fit")
    partner = {"fit": f + 1 - 2 * lax.rem(f, 2)}
    half = sum(sizes)
    count = len(sizes)
    pieces = range(count)
    mine = lax.rem(f, 2) * half
    theirs = half - mine
    me = r * C + c
    greet(("row", "col", "fit"))
    out = Sender(send_sems)
    offsets = [sum(sizes[:piece]) for piece in pieces]

    def place(piece, group, base=mine):
        return tiles.at[group, pl.ds(base + offsets[piece], sizes[piece])]

    def await_copy(piece, group, sem, base=mine, when=None):
        ref = place(piece, group, base)
        copy = pltpu.make_async_remote_copy(
            src_ref=ref, dst_ref=ref, send_sem=send_sems.at[0], recv_sem=sem,
            device_id=partner, device_id_type=MESH,
        )
        guarded(when, copy.wait_recv)

    def along(piece, group, step, when=None, source=None):
        inside = c + 1 < C if step > 0 else c > 0
        out.send(
            place(piece, group) if source is None else source, place(piece, group),
            recv_sems.at[piece, group], {"col": c + step}, both(when, inside),
        )

    def across(piece, group, when=None, source=None):
        for step in range(1, R):
            out.send(
                place(piece, group) if source is None else source, place(piece, group),
                recv_sems.at[piece, group], {"row": lax.rem(r + step, R)}, when,
            )

    def beside(piece, group, when=None):
        out.send(place(piece, group), place(piece, group), part_sems.at[piece, group], partner, when)

    def own_piece(piece):
        return own.at[pl.ds(mine + offsets[piece], sizes[piece])]

    for piece in pieces:
        for step in (1, -1):
            along(piece, me, step, source=own_piece(piece))
        across(piece, me, source=own_piece(piece))
    if with_ints:
        def int_wait(target, sem, when=None):
            copy = pltpu.make_async_remote_copy(
                src_ref=target, dst_ref=target, send_sem=send_sems.at[0], recv_sem=sem,
                device_id=partner, device_id_type=MESH,
            )
            guarded(when, copy.wait_recv)

        for step in (1, -1):
            inside = c + 1 < C if step > 0 else c > 0
            out.send(ints, row_ints.at[c], int_sems.at[0, c], {"col": c + step}, inside)
        for step in range(1, R):
            to = {"row": lax.rem(r + step, R)}
            out.send(ints, col_ints.at[r], int_sems.at[1, r], to)
            out.send(energy, col_en.at[r], int_sems.at[3, r], to)
        for step in range(1, C):
            to = {"col": lax.rem(c + step, C)}
            out.send(energy, row_en.at[c], int_sems.at[2, c], to)
    local = [pltpu.make_async_copy(own, tiles.at[me], local_sems.at[0])]
    if with_ints:
        local += [
            pltpu.make_async_copy(ints, row_ints.at[c], local_sems.at[1]),
            pltpu.make_async_copy(ints, col_ints.at[r], local_sems.at[2]),
            pltpu.make_async_copy(energy, row_en.at[c], local_sems.at[3]),
            pltpu.make_async_copy(energy, col_en.at[r], local_sems.at[4]),
        ]
    for copy in local:
        copy.start()
    events = []

    def behind(step, distance):
        source = c - step * distance
        there = jnp.logical_and(source >= 0, source < C)
        return jnp.clip(source, 0, C - 1), there

    def arrival(piece, step, distance):
        column, there = behind(step, distance)
        group = r * C + column
        await_copy(piece, group, recv_sems.at[piece, group], when=there)
        if distance < C - 1:
            along(piece, group, step, there)
        across(piece, group, there)
        beside(piece, group, there)

    def crossed(piece, other, step, distance):
        column, there = behind(step, distance)
        group = lax.rem(r + other, R) * C + column
        await_copy(piece, group, recv_sems.at[piece, group], when=there)
        beside(piece, group, there)

    def int_arrival(step, distance):
        column, there = behind(step, distance)
        int_wait(row_ints.at[column], int_sems.at[0, column], there)
        if distance < C - 1:
            inside = c + 1 < C if step > 0 else c > 0
            out.send(
                row_ints.at[column], row_ints.at[column], int_sems.at[0, column],
                {"col": c + step}, both(there, inside),
            )

    for piece in pieces:
        for other in range(1, R):
            events.append((1.5, piece, functools.partial(crossed, piece, other, 1, 0)))
        for distance in range(1, C):
            for step in (1, -1):
                events.append((distance, piece, functools.partial(arrival, piece, step, distance)))
                for other in range(1, R):
                    events.append((
                        distance + 1.5, piece, functools.partial(crossed, piece, other, step, distance)
                    ))
    if with_ints:
        for distance in range(1, C):
            for step in (1, -1):
                events.append((distance, count, functools.partial(int_arrival, step, distance)))
    for _, _, event in sorted(events, key=lambda entry: entry[:2]):
        event()
    if with_ints:
        for step in range(1, R):
            row = lax.rem(r + step, R)
            int_wait(col_ints.at[row], int_sems.at[1, row])
            int_wait(col_en.at[row], int_sems.at[3, row])
        for step in range(1, C):
            column = lax.rem(c + step, C)
            int_wait(row_en.at[column], int_sems.at[2, column])
    for step in range(1, R * C):
        group = lax.rem(me + step, R * C)
        for piece in pieces:
            await_copy(piece, group, part_sems.at[piece, group], base=theirs)
    for copy in local:
        copy.wait()
    out.finish()


def gather(packed, collective_id, ints=None, energy=None):
    R, C = lax.axis_size("row"), lax.axis_size("col")
    G = R * C
    with_ints = ints is not None
    half = packed.shape[0] // 2
    count = min(2, half)
    sizes = tuple(len(range(i, half, count)) for i in range(count))
    shapes = [jax.ShapeDtypeStruct((G,) + packed.shape, packed.dtype)]
    operands = [packed]
    if with_ints:
        operands += [ints, energy]
        shapes += [
            jax.ShapeDtypeStruct((C,) + ints.shape, ints.dtype),
            jax.ShapeDtypeStruct((R,) + ints.shape, ints.dtype),
            jax.ShapeDtypeStruct((C,) + energy.shape, energy.dtype),
            jax.ShapeDtypeStruct((R,) + energy.shape, energy.dtype),
        ]
    scratch = [
        pltpu.SemaphoreType.DMA((8 * len(sizes) * G + 32,)),
        pltpu.SemaphoreType.DMA((len(sizes), G)),
        pltpu.SemaphoreType.DMA((len(sizes), G)),
    ]
    if with_ints:
        scratch.append(pltpu.SemaphoreType.DMA((4, max(R, C))))
    scratch.append(pltpu.SemaphoreType.DMA((5,)))
    return pl.pallas_call(
        functools.partial(gather_kernel, sizes, with_ints),
        out_shape=shapes,
        in_specs=[ANY] * len(operands),
        out_specs=[ANY] * len(shapes),
        scratch_shapes=scratch,
        name="gather_ints" if with_ints else "gather_tiles",
        compiler_params=pltpu.CompilerParams(
            collective_id=collective_id, has_side_effects=True, vmem_limit_bytes=VMEM_LIMIT
        ),
    )(*operands)


def sum_kernel(part, total, inbox, result, send_sems, recv_sems, gather_sems, local_sem):
    F = lax.axis_size("fit")
    f = lax.axis_index("fit")
    rows = part.shape[0] // F
    greet(("fit",))
    out = Sender(send_sems)
    for step in range(1, F):
        to = lax.rem(f + step, F)
        out.send(
            part.at[pl.ds(to * rows, rows)], inbox.at[step - 1], recv_sems.at[step - 1], {"fit": to}
        )
    value = part[pl.ds(f * rows, rows)].astype(jnp.float32)
    for step in range(1, F):
        pltpu.make_async_remote_copy(
            src_ref=inbox.at[step - 1], dst_ref=inbox.at[step - 1], send_sem=send_sems.at[0],
            recv_sem=recv_sems.at[step - 1], device_id={"fit": lax.rem(f + step, F)},
            device_id_type=MESH,
        ).wait_recv()
        value = value + inbox[step - 1].astype(jnp.float32)
    result[...] = value.astype(result.dtype)
    target = total.at[pl.ds(f * rows, rows)]
    for step in range(1, F):
        out.send(result, target, gather_sems.at[step - 1], {"fit": lax.rem(f + step, F)})
    local = pltpu.make_async_copy(result, target, local_sem)
    local.start()
    for step in range(1, F):
        source = lax.rem(f + F - step, F)
        ref = total.at[pl.ds(source * rows, rows)]
        pltpu.make_async_remote_copy(
            src_ref=ref, dst_ref=ref, send_sem=send_sems.at[0], recv_sem=gather_sems.at[step - 1],
            device_id={"fit": source}, device_id_type=MESH,
        ).wait_recv()
    local.wait()
    out.finish()


def fit_sum(part, collective_id):
    F = lax.axis_size("fit")
    piece = (part.shape[0] // F,) + part.shape[1:]
    return pl.pallas_call(
        sum_kernel,
        out_shape=jax.ShapeDtypeStruct(part.shape, part.dtype),
        in_specs=[pl.BlockSpec(memory_space=pltpu.VMEM)],
        out_specs=ANY,
        scratch_shapes=[
            pltpu.VMEM((F - 1,) + piece, part.dtype),
            pltpu.VMEM(piece, part.dtype),
            pltpu.SemaphoreType.DMA((2 * F,)),
            pltpu.SemaphoreType.DMA((F,)),
            pltpu.SemaphoreType.DMA((F,)),
            pltpu.SemaphoreType.DMA,
        ],
        name="fit_sum",
        compiler_params=pltpu.CompilerParams(collective_id=collective_id, has_side_effects=True),
    )(part)


def couple_kernel(
    block, pair_count, first_turn, seconds, row_ref, shift_ref, fock_ref, first_ref, second_ref, tiles, inter, base,
    out, *kept
):
    links, size = inter.shape[1], inter.shape[2]
    first = pl.program_id(0) * block
    halves, results = [], []
    for q in range(block):
        for k in range(links):
            n = k * pair_count + first + q
            tile = pltpu.roll(tiles[row_ref[n]], shift_ref[n], 1)[:, :size]
            halves.append(jnp.dot(inter[q, k], tile, preferred_element_type=jnp.float32))
    for q in range(block):
        for k in range(links):
            scale = fock_ref[k * pair_count + first + q]
            halves[q * links + k] = (halves[q * links + k] * scale).astype(jnp.bfloat16)
    for q in range(block):
        results.append(
            sum(
                lax.dot_general(
                    halves[q * links + k], inter[q, k], (((1,), (1,)), ((), ())),
                    preferred_element_type=jnp.float32,
                )
                for k in range(links)
            )
        )
    for q in range(block):
        if first_turn:
            kept[0][q] = results[q]
            pick = first_ref[first + q] * seconds + second_ref[first + q]
            out[q] = (base[pick] - results[q]).astype(out.dtype)
        else:
            out[q] = (base[q] - results[q]).astype(out.dtype)


def couple(first_turn, seconds, rows, shifts, fock, firsts, others, tiles, inter, base):
    pair_count, links, size, _ = inter.shape
    block = math.gcd(pair_count, 32)
    smem = pl.BlockSpec(memory_space=pltpu.SMEM)
    whole = lambda shape: pl.BlockSpec(shape, lambda i: (0, 0, 0), pipeline_mode=pl.Buffered(1))
    by_pair = pl.BlockSpec((block, size, size), lambda i: (i, 0, 0))
    shapes = [jax.ShapeDtypeStruct((pair_count, size, size), jnp.bfloat16)]
    if first_turn:
        shapes.append(jax.ShapeDtypeStruct((pair_count, size, size), jnp.float32))
    return pl.pallas_call(
        functools.partial(couple_kernel, block, pair_count, first_turn, seconds),
        grid=(pair_count // block,),
        out_shape=shapes,
        in_specs=[
            smem, smem, smem, smem, smem,
            whole(tiles.shape),
            pl.BlockSpec((block, links, size, size), lambda i: (i, 0, 0, 0)),
            whole(base.shape) if first_turn else by_pair,
        ],
        out_specs=[by_pair] * len(shapes),
        name="couple",
        compiler_params=pltpu.CompilerParams(vmem_limit_bytes=VMEM_LIMIT),
    )(rows, shifts, fock, firsts, others, tiles, inter, base)


def on_device(
    orbital_ints,
    occ_energy,
    pair_row,
    pair_col,
    virt_energy,
    amplitudes,
    intersections,
    coupling_fock,
    partner_owner,
    partner_slot,
):
    R, C = lax.axis_size("row"), lax.axis_size("col")
    G = R * C
    size = amplitudes.shape[0]
    pair_count = amplitudes.shape[2]
    occ_block = occ_energy.shape[0]
    pack = LANES // size
    depth = -(-pair_count // pack)
    depth += -depth % 4
    direct = G <= 16

    def packed_tiles(current):
        tiles = jnp.transpose(current.astype(jnp.bfloat16), (2, 0, 1))
        tiles = jnp.pad(tiles, ((0, pack * depth - pair_count), (0, 0), (0, 0)))
        parts = [tiles[t * depth : (t + 1) * depth] for t in range(pack)]
        spare = jnp.zeros((depth, size, LANES - pack * size), jnp.bfloat16)
        return jnp.concatenate(parts + [spare], axis=2)

    packed = packed_tiles(amplitudes)
    if direct:
        energy = jnp.pad(occ_energy[None, :], ((0, 7), (0, LANES - occ_block)))
        tiles, row_ints, col_ints, row_en, col_en = gather(packed, 1, orbital_ints, energy)
        row_energy = row_en[:, 0, :occ_block].reshape(-1)
        col_energy = col_en[:, 0, :occ_block].reshape(-1)
        row_ints = row_ints.reshape((-1,) + orbital_ints.shape[1:])
        col_ints = col_ints.reshape((-1,) + orbital_ints.shape[1:])
    else:
        tiles = lax.all_gather(packed, ("row", "col"), axis=0)
        row_ints = lax.all_gather(orbital_ints, "col", axis=0, tiled=True)
        col_ints = lax.all_gather(orbital_ints, "row", axis=0, tiled=True)
        row_energy = lax.all_gather(occ_energy, "col", axis=0, tiled=True)
        col_energy = lax.all_gather(occ_energy, "row", axis=0, tiled=True)
    seconds = col_ints.shape[0]
    exchange = jnp.einsum(
        "iax,jbx->ijab", row_ints, col_ints, preferred_element_type=jnp.float32
    ).reshape(-1, size, size)
    first_hot = (pair_row[:, None] == jnp.arange(row_energy.shape[0])[None, :])
    second_hot = (pair_col[:, None] == jnp.arange(seconds)[None, :])
    occupied = jnp.sum(jnp.where(first_hot, row_energy[None, :], 0.0), axis=1) + jnp.sum(
        jnp.where(second_hot, col_energy[None, :], 0.0), axis=1
    )
    denominator = virt_energy[:, None, :] + virt_energy[None, :, :] - occupied[None, None, :]
    owners = partner_owner[0].T.reshape(-1)
    slots = partner_slot[0].T.reshape(-1)
    turn = sum((slots >= t * depth).astype(jnp.int32) for t in range(1, pack))
    rows = owners * depth + slots - turn * depth
    shifts = jnp.where(turn == 0, 0, LANES - turn * size)
    fock = coupling_fock.reshape(-1)
    inter = jnp.transpose(intersections, (3, 2, 0, 1))
    current = amplitudes
    residual = amplitudes
    base = exchange
    for step in range(ITERS):
        if step > 0:
            packed = packed_tiles(current)
            if direct:
                (tiles,) = gather(packed, 2)
            else:
                tiles = lax.all_gather(packed, ("row", "col"), axis=0)
        tiles = tiles.reshape(G * depth, size, LANES)
        part, *kept = couple(
            step == 0, seconds, rows, shifts, fock, pair_row, pair_col, tiles, inter, base
        )
        change = fit_sum(jnp.transpose(part, (1, 2, 0)), 3).astype(jnp.float32)
        if step == 0:
            base = kept[0]
            total = change
        else:
            total = total + change
        residual = total + denominator * current
        current = current - residual / denominator
    return (current, residual)


def solution(mesh):
    placed = (
        P(("row", "col"), None, "fit"),
        P(("row", "col")),
        P(("row", "col")),
        P(("row", "col")),
        P(None, ("row", "col")),
        P(None, None, ("row", "col")),
        P(None, None, "fit", ("row", "col")),
        P("fit", ("row", "col")),
        P("fit", ("row", "col"), None),
        P("fit", ("row", "col"), None),
    )
    out = P(None, None, ("row", "col"))
    return jax.shard_map(
        on_device, mesh=mesh, in_specs=placed, out_specs=(out, out), check_vma=False
    )
```
